512 devices in a mesh: vox: 512 (over y, z, x, core).
Axes of the slice: x: 4, y: 4, z: 16, core: 2. Of those that a mesh axis runs over, the one named last changes fastest.
Arguments:
- deform: bfloat16 [1048576, 1024], P('vox'), may hold values from -8 to 8
- sketch: bfloat16 [1024, 256], replicated, may hold values from -0.1875 to 0.1875
Outputs:
- factor_r: float32 [256, 256], replicated
- projected: float32 [1024, 256], P('vox')
The draws below stay inside these ranges and needn't reach their ends.
All inputs are finite; a program needn't handle non-finite values.
Results may differ from the reference program's by a relative error of at most 0.0012.
Values sent between devices are 32-bit elements; how exact they have to be, the bound alone decides.
No kernel may reach another device: no remote copies, remote signals or barrier semaphores. Data moves between devices by JAX's collectives and lax.ppermute only.
A program may use at most 64 MiB of HBM per device.

```python
import jax
import jax.numpy as jnp
from jax import lax

NS = 1024
K = 256
TOTAL_ROWS = 1048576


def draw_deform(key, part):
    base = jax.random.fold_in(key, 11)
    key_a, key_b, key_c = jax.random.split(base, 3)
    noise = jax.random.normal(key_a, (TOTAL_ROWS, NS), jnp.float32)
    row_log = jax.random.uniform(key_b, (TOTAL_ROWS, 1), jnp.float32) * jnp.log(10.0)
    ramp = jnp.log(3.0) * jnp.arange(TOTAL_ROWS, dtype=jnp.float32)[:, None] / TOTAL_ROWS
    col_scale = jnp.exp(jax.random.uniform(key_c, (1, NS), jnp.float32) * jnp.log(10.0))
    values = noise * jnp.exp(row_log + ramp) * col_scale / 30.0
    return jnp.clip(values, -8.0, 8.0).astype(jnp.bfloat16)


def centred(stream_key, extent, deviation, most, kind=jnp.bfloat16):
    values = deviation * jax.random.normal(stream_key, extent, jnp.float32)
    return jnp.clip(values, min=-most, max=most).astype(kind)


def setup_inputs(seed: int = 0) -> dict:
    keys = jax.random.split(jax.random.key(seed), 3)
    return {
        "deform": draw_deform(jax.random.fold_in(keys[2], 71), 0),
        "sketch": centred(keys[1], (NS, K), NS ** -0.5, 0.1875),
    }


def reference(deform, sketch):
    sketched = jnp.dot(deform.astype(jnp.float32), sketch.astype(jnp.float32), preferred_element_type=jnp.float32)
    gram = lax.dot_general(sketched.astype(jnp.float32), sketched.astype(jnp.float32), (((0,), (0,)), ((), ())), precision=lax.Precision.HIGHEST, preferred_element_type=jnp.float32)
    lower = jnp.linalg.cholesky(gram)
    factor_r = lower.T * (1.0 / jnp.sqrt(jnp.float32(TOTAL_ROWS)))
    basis = lax.linalg.triangular_solve(lower, sketched, left_side=False, lower=True, transpose_a=True)
    high = basis.astype(jnp.bfloat16)
    rest = (basis - high.astype(jnp.float32)).astype(jnp.bfloat16)
    dims = (((0,), (0,)), ((), ()))
    projected = lax.dot_general(deform.astype(jnp.float32), high.astype(jnp.float32), dims, preferred_element_type=jnp.float32) + lax.dot_general(deform.astype(jnp.float32), rest.astype(jnp.float32), dims, preferred_element_type=jnp.float32)
    return (factor_r, projected)
```

```python
import functools

import jax
import jax.numpy as jnp
import numpy as np
from jax import lax
from jax.experimental import pallas as pl
from jax.experimental.pallas import tpu as pltpu
from jax.sharding import Mesh
from jax.sharding import PartitionSpec as P

NT = (((1,), (1,)), ((), ()))
def nt(a,b): return lax.dot_general(a,b,NT,precision=lax.Precision.HIGHEST,preferred_element_type=jnp.float32)

def lanes(v, k):
    return jnp.broadcast_to(v[:, k:k+1], (8, 128))
def rows(v, t):
    return jnp.broadcast_to(v[t:t+1, :], (8, 128))

def factor128(a):
    lane = lax.broadcasted_iota(jnp.int32, (8, 128), 1)
    sub = lax.broadcasted_iota(jnp.int32, (8, 128), 0)
    a = list(a)
    w = [jnp.where(lane == sub + 8*i, 1.0, 0.0) for i in range(16)]
    for j in range(0, 128, 2):
        b, t = divmod(j, 8)
        r0, r1 = rows(a[b], t), rows(a[b], t+1)
        w0, w1 = rows(w[b], t), rows(w[b], t+1)
        p, q, s = lanes(r0, j), lanes(r0, j+1), lanes(r1, j+1)
        inv = 1.0 / (p*s - q*q)
        pi, qi, si = p*inv, q*inv, s*inv
        u0, u1 = si*r0 - qi*r1, pi*r1 - qi*r0
        v0, v1 = si*w0 - qi*w1, pi*w1 - qi*w0
        for i in range(b, 16):
            if i == b and t == 6: continue
            c0, c1 = lanes(a[i], j), lanes(a[i], j+1)
            if i == b:
                m = sub > t+1
                c0, c1 = jnp.where(m, c0, 0.0), jnp.where(m, c1, 0.0)
            a[i] = a[i] - (c0*u0 + c1*u1)
            w[i] = w[i] - (c0*v0 + c1*v1)
    ro, wo = [], []
    odd = sub % 2 == 1
    for i in range(16):
        d = lane - (sub + 8*i)
        p = jnp.sum(jnp.where(d == 0, a[i], 0.0), axis=1, keepdims=True)
        q = jnp.sum(jnp.where(d == 1, a[i], 0.0), axis=1, keepdims=True)
        f = jnp.broadcast_to(q / p, (8, 128))
        f = jnp.where(odd, pltpu.roll(f, 1, 0), 0.0)
        x = a[i] - f*pltpu.roll(a[i], 1, 0)
        y = w[i] - f*pltpu.roll(w[i], 1, 0)
        p = jnp.sum(jnp.where(d == 0, x, 0.0), axis=1, keepdims=True)
        g = jnp.broadcast_to(lax.rsqrt(p), (8, 128))
        ro.append(jnp.where(d >= 0, x*g, 0.0))
        wo.append(y*g)
    return ro, wo

def blocks(x): return [x[8*i:8*i+8, :] for i in range(x.shape[0]//8)]
def cat(bs): return jnp.concatenate(bs, axis=0)

def chol_kernel(scale, g_ref, c_ref, r_ref, p_ref):
    lane = lax.broadcasted_iota(jnp.int32, (128, 128), 1)
    sub = lax.broadcasted_iota(jnp.int32, (128, 128), 0)
    eye = lane == sub
    a11, a21, a22 = g_ref[0:128, :], g_ref[128:256, :], g_ref[256:384, :]
    def diag(x):
        e = jnp.where(eye, x, 0.0)
        return jnp.sum(e, axis=0, keepdims=True), jnp.sum(e, axis=1, keepdims=True)
    l1, s1 = diag(a11); l2, s2 = diag(a22)
    il1, is1, il2, is2 = map(lax.rsqrt, (l1, s1, l2, s2))
    c1, c2 = c_ref[0:8, :] * il1, pltpu.roll(c_ref[...], 6, 0) * il2
    a11 = a11 * is1 * il1
    a21 = a21 * is2 * il1
    a22 = a22 * is2 * il2
    r11, w1 = factor128(blocks(a11))
    r_ref[0:128, 0:128] = cat(r11) * (l1 * il1 * scale)
    w1 = cat(w1)
    low = nt(cat([a21, c1]), w1)
    l21, p1 = low[0:128], low[128:136]
    r_ref[0:128, 128:256] = nt(w1, a21) * (l2 * il2 * scale)
    upd = nt(low, l21)
    a22 = a22 - upd[0:128]
    c2 = c2 - upd[128:136]
    r22, w2 = factor128(blocks(a22))
    p2 = nt(c2, cat(w2))
    r_ref[128:256, 0:128] = jnp.zeros((128, 128), jnp.float32)
    r_ref[128:256, 128:256] = cat(r22) * (l2 * il2 * scale)
    p_ref[:, 0:128] = p1[0:2]
    p_ref[:, 128:256] = p2[0:2]

def chol(g, c, scale, **kw):
    return pl.pallas_call(functools.partial(chol_kernel, scale),
        out_shape=(jax.ShapeDtypeStruct((256,256),jnp.float32), jax.ShapeDtypeStruct((2,256),jnp.float32)), **kw)(g, c)

TN_NT = (((0,), (1,)), ((), ()))
GRAM_ROWS = 24
CROSS_ROWS = 64
PLANE = 16
RING = 16


def front_kernel(core_ref, deform_ref, sketch_ref, keep_ref, send_ref, cross_acc, gram_acc, lines):
    step = pl.program_id(0)
    deform = deform_ref[...]
    sketched = lax.dot_general(sketch_ref[...], deform, TN_NT, preferred_element_type=jnp.float32)
    high = sketched.astype(jnp.bfloat16)
    rest = (sketched - high.astype(jnp.float32)).astype(jnp.bfloat16)
    pair = jnp.concatenate([high, rest], axis=0)
    cross = jnp.dot(pair, deform, preferred_element_type=jnp.float32)
    cross = cross[:256] + cross[256:]
    gram = lax.dot_general(pair, high, NT, preferred_element_type=jnp.float32)

    @pl.when(step == 0)
    def _():
        cross_acc[...] = cross
        gram_acc[...] = gram

    @pl.when(step > 0)
    def _():
        cross_acc[...] += cross
        gram_acc[...] += gram

    @pl.when(step == pl.num_programs(0) - 1)
    def _():
        mixed = gram_acc[256:512, :]
        whole = gram_acc[0:256, :] + mixed + mixed.T
        packed = jnp.concatenate([whole[0:128, 0:128], whole[128:256, 0:128], whole[128:256, 128:256]], axis=0)
        for peer in range(PLANE):
            part = packed[peer * GRAM_ROWS : (peer + 1) * GRAM_ROWS]
            keep_ref[peer, 0:GRAM_ROWS, :] = part
            send_ref[peer, 0:GRAM_ROWS, :] = part
        for half in range(2):
            for block in range(8):
                tile = cross_acc[half * 128 : half * 128 + 128, block * 128 : block * 128 + 128]
                lines[half, block * 128 : block * 128 + 128, :] = tile.T
        core = core_ref[0]
        for peer in range(PLANE):
            y, x = divmod(peer, 4)
            for half in range(2):
                for i in range(2):
                    at = GRAM_ROWS + (half * 2 + i) * RING
                    base = y * 256 + x * 4 + i
                    keep_ref[peer, at : at + RING, :] = lines[half, pl.ds(base + core * 2, RING, stride=16), :]
                    send_ref[peer, at : at + RING, :] = lines[half, pl.ds(base + 2 - core * 2, RING, stride=16), :]


def front(deform, sketch, core, rows=2048):
    shape = jax.ShapeDtypeStruct((PLANE, GRAM_ROWS + CROSS_ROWS, 128), jnp.float32)
    whole = lambda *_: (0, 0, 0)
    return pl.pallas_call(
        front_kernel,
        grid_spec=pltpu.PrefetchScalarGridSpec(
            num_scalar_prefetch=1,
            grid=(deform.shape[0] // rows,),
            in_specs=[pl.BlockSpec((rows, 1024), lambda i, _: (i, 0)), pl.BlockSpec((1024, 256), lambda i, _: (0, 0))],
            out_specs=[pl.BlockSpec(shape.shape, whole)] * 2,
            scratch_shapes=[
                pltpu.VMEM((256, 1024), jnp.float32),
                pltpu.VMEM((512, 256), jnp.float32),
                pltpu.VMEM((2, 1024, 128), jnp.float32),
            ],
        ),
        out_shape=(shape, shape),
        compiler_params=pltpu.CompilerParams(vmem_limit_bytes=60 << 20),
        name="front",
    )(core, deform, sketch)


def plane_kernel(in_ref, out_ref):
    total = in_ref[0]
    for peer in range(1, PLANE):
        total = total + in_ref[peer]
    spare = jnp.zeros((4, 128), jnp.float32)
    for z in range(RING):
        out_ref[z * 32 : z * 32 + GRAM_ROWS, :] = total[0:GRAM_ROWS]
        out_ref[z * 32 + 28 : z * 32 + 32, :] = spare
    for q in range(4):
        at = GRAM_ROWS + q * RING
        out_ref[pl.ds(GRAM_ROWS + q, RING, stride=32), :] = total[at : at + RING]


def plane_sum(arrived):
    out = pl.pallas_call(
        plane_kernel,
        out_shape=jax.ShapeDtypeStruct((RING * 32, 128), jnp.float32),
        name="plane_sum",
    )(arrived)
    return out.reshape(RING, 32, 128)


def ring_kernel(in_ref, chunk_ref, own_ref):
    total = in_ref[0]
    for z in range(1, RING):
        total = total + in_ref[z]
    for peer in range(PLANE):
        chunk_ref[peer] = total[0:GRAM_ROWS]
    own_ref[...] = total[GRAM_ROWS:32]


def ring_sum(arrived):
    return pl.pallas_call(
        ring_kernel,
        out_shape=(
            jax.ShapeDtypeStruct((PLANE, GRAM_ROWS, 128), jnp.float32),
            jax.ShapeDtypeStruct((8, 128), jnp.float32),
        ),
        name="ring_sum",
    )(arrived)


def swap(values, axis):
    return lax.all_to_all(values, axis, split_axis=0, concat_axis=0, tiled=True)


def body(deform, sketch):
    core = lax.axis_index("c").astype(jnp.int32).reshape(1)
    keep, send = front(deform, sketch, core)
    chip = keep + lax.ppermute(send, "c", [(0, 1), (1, 0)])
    own_plane = plane_sum(swap(chip, ("y", "x")))
    chunks, own = ring_sum(swap(own_plane, ("z",)))
    packed = swap(chunks, ("y", "x")).reshape(384, 128)
    total_rows = deform.shape[0] * lax.axis_size(("y", "z", "x", "c"))
    return chol(packed, own, 1.0 / float(np.sqrt(np.float32(total_rows))))


def solution(mesh):
    split = Mesh(mesh.devices.reshape(4, 16, 4, 2), ("y", "z", "x", "c"))
    axes = ("y", "z", "x", "c")
    in_specs = (P(axes, None), P())
    out_specs = (P(), P(axes, None))
    return jax.shard_map(body, mesh=split, in_specs=in_specs, out_specs=out_specs, check_vma=False)
```

```python
import functools

import jax
import jax.numpy as jnp
import numpy as np
from jax import lax
from jax.experimental import pallas as pl
from jax.experimental.pallas import tpu as pltpu
from jax.sharding import Mesh
from jax.sharding import PartitionSpec as P

NT = (((1,), (1,)), ((), ()))
def nt(a,b): return lax.dot_general(a,b,NT,precision=lax.Precision.HIGHEST,preferred_element_type=jnp.float32)

def lanes(v, k):
    return jnp.broadcast_to(v[:, k:k+1], (8, 128))
def rows(v, t):
    return jnp.broadcast_to(v[t:t+1, :], (8, 128))

def factor128(a):
    lane = lax.broadcasted_iota(jnp.int32, (8, 128), 1)
    sub = lax.broadcasted_iota(jnp.int32, (8, 128), 0)
    a = list(a)
    w = [jnp.where(lane == sub + 8*i, 1.0, 0.0) for i in range(16)]
    fa, fw = [], []
    for b in range(16):
        x = [lanes(a[b], 8*b+k) for k in range(8)] + [a[b], w[b]]
        f = [a[b], w[b]]
        for t in range(0, 8, 2):
            if t:
                late = sub >= t
                f = [jnp.where(late, n, o) for n, o in zip(x[8:], f)]
            c0, c1 = x[t], x[t+1]
            p, q, s = rows(c0, t), rows(c0, t+1), rows(c1, t+1)
            inv = 1.0 / (p*s - q*q)
            pi, qi, si = p*inv, q*inv, s*inv
            for k in range(t+2, 10):
                r0, r1 = rows(x[k], t), rows(x[k], t+1)
                u0, u1 = si*r0 - qi*r1, pi*r1 - qi*r0
                new = x[k] - (c0*u0 + c1*u1)
                x[k] = jnp.where(sub == t, u0, jnp.where(sub == t+1, u1, new))
        fa.append(f[0]); fw.append(f[1])
        ga = [rows(x[8], k) for k in range(8)]
        gw = [rows(x[9], k) for k in range(8)]
        for i in range(b+1, 16):
            c = [lanes(a[i], 8*b+k) for k in range(8)]
            a[i] = a[i] - tree([c[k]*ga[k] for k in range(8)])
            w[i] = w[i] - tree([c[k]*gw[k] for k in range(8)])
    a, w = fa, fw
    ro, wo = [], []
    odd = sub % 2 == 1
    for i in range(16):
        d = lane - (sub + 8*i)
        p = jnp.sum(jnp.where(d == 0, a[i], 0.0), axis=1, keepdims=True)
        q = jnp.sum(jnp.where(d == 1, a[i], 0.0), axis=1, keepdims=True)
        f = jnp.broadcast_to(q / p, (8, 128))
        f = jnp.where(odd, pltpu.roll(f, 1, 0), 0.0)
        x = a[i] - f*pltpu.roll(a[i], 1, 0)
        y = w[i] - f*pltpu.roll(w[i], 1, 0)
        p = jnp.sum(jnp.where(d == 0, x, 0.0), axis=1, keepdims=True)
        g = jnp.broadcast_to(lax.rsqrt(p), (8, 128))
        ro.append(jnp.where(d >= 0, x*g, 0.0))
        wo.append(y*g)
    return ro, wo

def tree(v):
    while len(v) > 1: v = [v[n] + v[n+1] for n in range(0, len(v), 2)]
    return v[0]

def blocks(x): return [x[8*i:8*i+8, :] for i in range(x.shape[0]//8)]
def cat(bs): return jnp.concatenate(bs, axis=0)

def chol_kernel(scale, g_ref, c_ref, r_ref, p_ref):
    lane = lax.broadcasted_iota(jnp.int32, (128, 128), 1)
    sub = lax.broadcasted_iota(jnp.int32, (128, 128), 0)
    eye = lane == sub
    a11, a21, a22 = g_ref[0:128, :], g_ref[128:256, :], g_ref[256:384, :]
    def diag(x):
        e = jnp.where(eye, x, 0.0)
        return jnp.sum(e, axis=0, keepdims=True), jnp.sum(e, axis=1, keepdims=True)
    l1, s1 = diag(a11); l2, s2 = diag(a22)
    il1, is1, il2, is2 = map(lax.rsqrt, (l1, s1, l2, s2))
    c1, c2 = c_ref[0:8, :] * il1, pltpu.roll(c_ref[...], 6, 0) * il2
    a11 = a11 * is1 * il1
    a21 = a21 * is2 * il1
    a22 = a22 * is2 * il2
    r11, w1 = factor128(blocks(a11))
    r_ref[0:128, 0:128] = cat(r11) * (l1 * il1 * scale)
    w1 = cat(w1)
    low = nt(cat([a21, c1]), w1)
    l21, p1 = low[0:128], low[128:136]
    r_ref[0:128, 128:256] = nt(w1, a21) * (l2 * il2 * scale)
    upd = nt(low, l21)
    a22 = a22 - upd[0:128]
    c2 = c2 - upd[128:136]
    r22, w2 = factor128(blocks(a22))
    p2 = nt(c2, cat(w2))
    r_ref[128:256, 0:128] = jnp.zeros((128, 128), jnp.float32)
    r_ref[128:256, 128:256] = cat(r22) * (l2 * il2 * scale)
    p_ref[:, 0:128] = p1[0:2]
    p_ref[:, 128:256] = p2[0:2]

def chol(g, c, scale, **kw):
    return pl.pallas_call(functools.partial(chol_kernel, scale),
        out_shape=(jax.ShapeDtypeStruct((256,256),jnp.float32), jax.ShapeDtypeStruct((2,256),jnp.float32)), **kw)(g, c)

TN_NT = (((0,), (1,)), ((), ()))
GRAM_ROWS = 24
CROSS_ROWS = 64
PLANE = 16
RING = 16
ROWS = 2048
CHUNKS = 4
SMALL = pltpu.CompilerParams(vmem_limit_bytes=8 << 20)


def front_kernel(core_ref, deform_hbm, sketch_hbm, keep_ref, send_ref, deform, sketch, pair, lines, sems):
    span = ROWS // CHUNKS
    load = pltpu.make_async_copy(sketch_hbm, sketch, sems.at[CHUNKS])
    load.start()
    loads = []
    for n in range(CHUNKS):
        part = pl.ds(n * span, span)
        loads.append(pltpu.make_async_copy(deform_hbm.at[part], deform.at[part], sems.at[n]))
        loads[-1].start()
    load.wait()
    for n in range(CHUNKS):
        loads[n].wait()
        part = slice(n * span, (n + 1) * span)
        sketched = lax.dot_general(sketch[...], deform[part], TN_NT, preferred_element_type=jnp.float32)
        high = sketched.astype(jnp.bfloat16)
        pair[0:256, part] = high
        pair[256:512, part] = (sketched - high.astype(jnp.float32)).astype(jnp.bfloat16)
    gram = lax.dot_general(pair[...], pair[0:256, :], NT, preferred_element_type=jnp.float32)
    mixed = gram[256:512]
    whole = gram[0:256] + mixed + mixed.T
    packed = jnp.concatenate([whole[0:128, 0:128], whole[128:256, 0:128], whole[128:256, 128:256]], axis=0)
    for peer in range(PLANE):
        part = packed[peer * GRAM_ROWS : (peer + 1) * GRAM_ROWS]
        keep_ref[peer, 0:GRAM_ROWS, :] = part
        send_ref[peer, 0:GRAM_ROWS, :] = part
    core = core_ref[0]
    for y in range(4):
        cols = slice(y * 256, y * 256 + 256)
        cross = jnp.dot(pair[...], deform[:, cols], preferred_element_type=jnp.float32)
        cross = cross[0:256] + cross[256:512]
        for half in range(2):
            for block in range(2):
                at = y * 256 + block * 128
                tile = cross[half * 128 : half * 128 + 128, block * 128 : block * 128 + 128]
                lines[half, at : at + 128, :] = tile.T
        for x in range(4):
            for half in range(2):
                for i in range(2):
                    at = GRAM_ROWS + (half * 2 + i) * RING
                    base = y * 256 + x * 4 + i
                    keep_ref[y * 4 + x, at : at + RING, :] = lines[half, pl.ds(base + core * 2, RING, stride=16), :]
                    send_ref[y * 4 + x, at : at + RING, :] = lines[half, pl.ds(base + 2 - core * 2, RING, stride=16), :]


def front(deform, sketch, core):
    shape = jax.ShapeDtypeStruct((PLANE, GRAM_ROWS + CROSS_ROWS, 128), jnp.float32)
    return pl.pallas_call(
        front_kernel,
        in_specs=[pl.BlockSpec(memory_space=pltpu.SMEM)] + [pl.BlockSpec(memory_space=pltpu.HBM)] * 2,
        out_specs=[pl.BlockSpec(memory_space=pltpu.VMEM)] * 2,
        scratch_shapes=[
            pltpu.VMEM((ROWS, 1024), jnp.bfloat16),
            pltpu.VMEM((1024, 256), jnp.bfloat16),
            pltpu.VMEM((512, ROWS), jnp.bfloat16),
            pltpu.VMEM((2, 1024, 128), jnp.float32),
            pltpu.SemaphoreType.DMA((CHUNKS + 1,)),
        ],
        out_shape=(shape, shape),
        compiler_params=pltpu.CompilerParams(vmem_limit_bytes=32 << 20),
        name="front",
    )(core, pltpu.with_memory_space_constraint(deform, pltpu.HBM), pltpu.with_memory_space_constraint(sketch, pltpu.HBM))


def plane_kernel(in_ref, out_ref):
    total = in_ref[0]
    for peer in range(1, PLANE):
        total = total + in_ref[peer]
    spare = jnp.zeros((4, 128), jnp.float32)
    for z in range(RING):
        out_ref[z * 32 : z * 32 + GRAM_ROWS, :] = total[0:GRAM_ROWS]
        out_ref[z * 32 + 28 : z * 32 + 32, :] = spare
    for q in range(4):
        at = GRAM_ROWS + q * RING
        out_ref[pl.ds(GRAM_ROWS + q, RING, stride=32), :] = total[at : at + RING]


def plane_sum(arrived):
    out = pl.pallas_call(
        plane_kernel,
        out_shape=jax.ShapeDtypeStruct((RING * 32, 128), jnp.float32),
        compiler_params=SMALL,
        name="plane_sum",
    )(arrived)
    return out.reshape(RING, 32, 128)


def ring_kernel(in_ref, chunk_ref, own_ref):
    total = in_ref[0]
    for z in range(1, RING):
        total = total + in_ref[z]
    for peer in range(PLANE):
        chunk_ref[peer] = total[0:GRAM_ROWS]
    own_ref[...] = total[GRAM_ROWS:32]


def ring_sum(arrived):
    return pl.pallas_call(
        ring_kernel,
        out_shape=(
            jax.ShapeDtypeStruct((PLANE, GRAM_ROWS, 128), jnp.float32),
            jax.ShapeDtypeStruct((8, 128), jnp.float32),
        ),
        compiler_params=SMALL,
        name="ring_sum",
    )(arrived)


def swap(values, axis):
    return lax.all_to_all(values, axis, split_axis=0, concat_axis=0, tiled=True)


def body(deform, sketch):
    core = lax.axis_index("c").astype(jnp.int32).reshape(1)
    keep, send = front(deform, sketch, core)
    chip = keep + lax.ppermute(send, "c", [(0, 1), (1, 0)])
    own_plane = plane_sum(swap(chip, ("y", "x")))
    chunks, own = ring_sum(swap(own_plane, ("z",)))
    packed = swap(chunks, ("y", "x")).reshape(384, 128)
    total_rows = deform.shape[0] * lax.axis_size(("y", "z", "x", "c"))
    return chol(packed, own, 1.0 / float(np.sqrt(np.float32(total_rows))), compiler_params=SMALL, name="factor")


def solution(mesh):
    split = Mesh(mesh.devices.reshape(4, 16, 4, 2), ("y", "z", "x", "c"))
    axes = ("y", "z", "x", "c")
    in_specs = (P(axes, None), P())
    out_specs = (P(), P(axes, None))
    return jax.shard_map(body, mesh=split, in_specs=in_specs, out_specs=out_specs, check_vma=False)
```

```python
import functools

import jax
import jax.numpy as jnp
import numpy as np
from jax import lax
from jax.experimental import pallas as pl
from jax.experimental.pallas import tpu as pltpu
from jax.sharding import Mesh
from jax.sharding import PartitionSpec as P

NT = (((1,), (1,)), ((), ()))
def nt(a,b): return lax.dot_general(a,b,NT,precision=lax.Precision.HIGHEST,preferred_element_type=jnp.float32)

def lanes(v, k):
    return jnp.broadcast_to(v[:, k:k+1], (8, 128))
def rows(v, t):
    return jnp.broadcast_to(v[t:t+1, :], (8, 128))

def factor128(a):
    lane = lax.broadcasted_iota(jnp.int32, (8, 128), 1)
    sub = lax.broadcasted_iota(jnp.int32, (8, 128), 0)
    a = list(a)
    w = [jnp.where(lane == sub + 8*i, 1.0, 0.0) for i in range(16)]
    fa, fw = [], []
    todo = []
    for b in range(16):
        x = [jnp.where(lane < 128 + k, lanes(a[b], 8*b+k), 1.0) for k in range(8)] + [a[b], w[b]]
        f = [None, None]
        share = -(-len(todo) // 4)
        for t in range(0, 8, 2):
            c0, c1 = x[t], x[t+1]
            p, q, s = rows(c0, t), rows(c0, t+1), rows(c1, t+1)
            det = p*s - q*q
            inv = 1.0 / det
            g0 = lax.rsqrt(p)
            g1 = p * lax.rsqrt(p * det)
            step = q * g0 * g0
            pi, qi, si = p*inv, q*inv, s*inv
            for k in range(t+2, 10):
                r0, r1 = rows(x[k], t), rows(x[k], t+1)
                if k >= 8:
                    y0, y1 = r0*g0, (r1 - step*r0)*g1
                    f[k-8] = jnp.where(sub == t, y0, y1) if t == 0 else jnp.where(sub < t, f[k-8], jnp.where(sub == t, y0, y1))
                u0, u1 = si*r0 - qi*r1, pi*r1 - qi*r0
                new = x[k] - (c0*u0 + c1*u1)
                x[k] = jnp.where(sub == t, u0, jnp.where(sub == t+1, u1, new))
            for work in todo[:share]: work()
            todo = todo[share:]
        for work in todo: work()
        fa.append(f[0]); fw.append(f[1])
        ga = [rows(x[8], k) for k in range(8)]
        gw = [rows(x[9], k) for k in range(8)]
        def update(i, b=b, ga=ga, gw=gw):
            c = [lanes(a[i], 8*b+k) for k in range(8)]
            a[i] = a[i] - tree([c[k]*ga[k] for k in range(8)])
            w[i] = w[i] - tree([c[k]*gw[k] for k in range(8)])
        if b < 15: update(b+1)
        todo = [functools.partial(update, i) for i in range(b+2, 16)]
    ro = [jnp.where(lane >= sub + 8*i, fa[i], 0.0) for i in range(16)]
    return ro, fw

def tree(v):
    while len(v) > 1: v = [v[n] + v[n+1] for n in range(0, len(v), 2)]
    return v[0]

def blocks(x): return [x[8*i:8*i+8, :] for i in range(x.shape[0]//8)]
def cat(bs): return jnp.concatenate(bs, axis=0)

def chol_kernel(scale, g_ref, c_ref, r_ref, p_ref):
    lane = lax.broadcasted_iota(jnp.int32, (128, 128), 1)
    sub = lax.broadcasted_iota(jnp.int32, (128, 128), 0)
    eye = lane == sub
    a11, a21, a22 = g_ref[0:128, :], g_ref[128:256, :], g_ref[256:384, :]
    def diag(x):
        e = jnp.where(eye, x, 0.0)
        return jnp.sum(e, axis=0, keepdims=True), jnp.sum(e, axis=1, keepdims=True)
    l1, s1 = diag(a11); l2, s2 = diag(a22)
    il1, is1, il2, is2 = map(lax.rsqrt, (l1, s1, l2, s2))
    c1, c2 = c_ref[0:8, :] * il1, pltpu.roll(c_ref[...], 6, 0) * il2
    a11 = a11 * is1 * il1
    a21 = a21 * is2 * il1
    a22 = a22 * is2 * il2
    r11, w1 = factor128(blocks(a11))
    r_ref[0:128, 0:128] = cat(r11) * (l1 * il1 * scale)
    w1 = cat(w1)
    low = nt(cat([a21, c1]), w1)
    l21, p1 = low[0:128], low[128:136]
    r_ref[0:128, 128:256] = nt(w1, a21) * (l2 * il2 * scale)
    upd = nt(low, l21)
    a22 = a22 - upd[0:128]
    c2 = c2 - upd[128:136]
    r22, w2 = factor128(blocks(a22))
    p2 = nt(c2, cat(w2))
    r_ref[128:256, 0:128] = jnp.zeros((128, 128), jnp.float32)
    r_ref[128:256, 128:256] = cat(r22) * (l2 * il2 * scale)
    p_ref[:, 0:128] = p1[0:2]
    p_ref[:, 128:256] = p2[0:2]

def chol(g, c, scale, **kw):
    return pl.pallas_call(functools.partial(chol_kernel, scale),
        out_shape=(jax.ShapeDtypeStruct((256,256),jnp.float32), jax.ShapeDtypeStruct((2,256),jnp.float32)), **kw)(g, c)

GRAM_ROWS = 24
CROSS_ROWS = 64
PLANE = 16
RING = 16
ROWS = 2048
CHUNKS = 2
SMALL = pltpu.CompilerParams(vmem_limit_bytes=8 << 20)


def front_kernel(core_ref, deform_hbm, sketch_hbm, keep_ref, send_ref, deform, sketch, pair, lines, flat, sems):
    span = ROWS // CHUNKS
    load = pltpu.make_async_copy(sketch_hbm, sketch, sems.at[CHUNKS])
    load.start()
    loads = []
    for n in range(CHUNKS):
        part = pl.ds(n * span, span)
        loads.append(pltpu.make_async_copy(deform_hbm.at[part], deform.at[part], sems.at[n]))
        loads[-1].start()
    load.wait()
    flat[...] = sketch[...].T
    for n in range(CHUNKS):
        loads[n].wait()
        part = slice(n * span, (n + 1) * span)
        sketched = lax.dot_general(flat[...], deform[part], NT, preferred_element_type=jnp.float32)
        high = sketched.astype(jnp.bfloat16)
        pair[0:256, part] = high
        pair[256:512, part] = (sketched - high.astype(jnp.float32)).astype(jnp.bfloat16)
    gram = lax.dot_general(pair[...], pair[0:256, :], NT, preferred_element_type=jnp.float32)
    mixed = gram[256:512]
    whole = gram[0:256] + mixed + mixed.T
    packed = jnp.concatenate([whole[0:128, 0:128], whole[128:256, 0:128], whole[128:256, 128:256]], axis=0)
    for peer in range(PLANE):
        part = packed[peer * GRAM_ROWS : (peer + 1) * GRAM_ROWS]
        keep_ref[peer, 0:GRAM_ROWS, :] = part
        send_ref[peer, 0:GRAM_ROWS, :] = part
    core = core_ref[0]
    for y in range(4):
        cols = slice(y * 256, y * 256 + 256)
        cross = jnp.dot(pair[...], deform[:, cols], preferred_element_type=jnp.float32)
        cross = cross[0:256] + cross[256:512]
        for half in range(2):
            for block in range(2):
                at = y * 256 + block * 128
                tile = cross[half * 128 : half * 128 + 128, block * 128 : block * 128 + 128]
                lines[half, at : at + 128, :] = tile.T
        for x in range(4):
            for half in range(2):
                for i in range(2):
                    at = GRAM_ROWS + (half * 2 + i) * RING
                    base = y * 256 + x * 4 + i
                    keep_ref[y * 4 + x, at : at + RING, :] = lines[half, pl.ds(base + core * 2, RING, stride=16), :]
                    send_ref[y * 4 + x, at : at + RING, :] = lines[half, pl.ds(base + 2 - core * 2, RING, stride=16), :]


def front(deform, sketch, core):
    shape = jax.ShapeDtypeStruct((PLANE, GRAM_ROWS + CROSS_ROWS, 128), jnp.float32)
    return pl.pallas_call(
        front_kernel,
        in_specs=[pl.BlockSpec(memory_space=pltpu.SMEM)] + [pl.BlockSpec(memory_space=pltpu.HBM)] * 2,
        out_specs=[pl.BlockSpec(memory_space=pltpu.VMEM)] * 2,
        scratch_shapes=[
            pltpu.VMEM((ROWS, 1024), jnp.bfloat16),
            pltpu.VMEM((1024, 256), jnp.bfloat16),
            pltpu.VMEM((512, ROWS), jnp.bfloat16),
            pltpu.VMEM((2, 1024, 128), jnp.float32),
            pltpu.VMEM((256, 1024), jnp.bfloat16),
            pltpu.SemaphoreType.DMA((CHUNKS + 1,)),
        ],
        out_shape=(shape, shape),
        compiler_params=pltpu.CompilerParams(vmem_limit_bytes=32 << 20),
        name="front",
    )(core, pltpu.with_memory_space_constraint(deform, pltpu.HBM), pltpu.with_memory_space_constraint(sketch, pltpu.HBM))


def plane_kernel(in_ref, out_ref):
    total = in_ref[0]
    for peer in range(1, PLANE):
        total = total + in_ref[peer]
    spare = jnp.zeros((4, 128), jnp.float32)
    for z in range(RING):
        out_ref[z * 32 : z * 32 + GRAM_ROWS, :] = total[0:GRAM_ROWS]
        out_ref[z * 32 + 28 : z * 32 + 32, :] = spare
    for q in range(4):
        at = GRAM_ROWS + q * RING
        out_ref[pl.ds(GRAM_ROWS + q, RING, stride=32), :] = total[at : at + RING]


def plane_sum(arrived):
    out = pl.pallas_call(
        plane_kernel,
        out_shape=jax.ShapeDtypeStruct((RING * 32, 128), jnp.float32),
        compiler_params=SMALL,
        name="plane_sum",
    )(arrived)
    return out.reshape(RING, 32, 128)


def ring_kernel(in_ref, chunk_ref, own_ref):
    total = in_ref[0]
    for z in range(1, RING):
        total = total + in_ref[z]
    for peer in range(PLANE):
        chunk_ref[peer] = total[0:GRAM_ROWS]
    own_ref[...] = total[GRAM_ROWS:32]


def ring_sum(arrived):
    return pl.pallas_call(
        ring_kernel,
        out_shape=(
            jax.ShapeDtypeStruct((PLANE, GRAM_ROWS, 128), jnp.float32),
            jax.ShapeDtypeStruct((8, 128), jnp.float32),
        ),
        compiler_params=SMALL,
        name="ring_sum",
    )(arrived)


def swap(values, axis):
    return lax.all_to_all(values, axis, split_axis=0, concat_axis=0, tiled=True)


def body(deform, sketch):
    core = lax.axis_index("c").astype(jnp.int32).reshape(1)
    keep, send = front(deform, sketch, core)
    chip = keep + lax.ppermute(send, "c", [(0, 1), (1, 0)])
    own_plane = plane_sum(swap(chip, ("y", "x")))
    chunks, own = ring_sum(swap(own_plane, ("z",)))
    packed = swap(chunks, ("y", "x")).reshape(384, 128)
    total_rows = deform.shape[0] * lax.axis_size(("y", "z", "x", "c"))
    return chol(packed, own, 1.0 / float(np.sqrt(np.float32(total_rows))), compiler_params=SMALL, name="factor")


def solution(mesh):
    split = Mesh(mesh.devices.reshape(4, 16, 4, 2), ("y", "z", "x", "c"))
    axes = ("y", "z", "x", "c")
    in_specs = (P(axes, None), P())
    out_specs = (P(), P(axes, None))
    return jax.shard_map(body, mesh=split, in_specs=in_specs, out_specs=out_specs, check_vma=False)
```

```python
import functools

import jax
import jax.numpy as jnp
import numpy as np
from jax import lax
from jax.experimental import pallas as pl
from jax.experimental.pallas import tpu as pltpu
from jax.sharding import Mesh
from jax.sharding import PartitionSpec as P

NT = (((1,), (1,)), ((), ()))
def nt(a,b): return lax.dot_general(a,b,NT,precision=lax.Precision.HIGHEST,preferred_element_type=jnp.float32)

def lanes(v, k):
    return jnp.broadcast_to(v[:, k:k+1], (8, 128))
def rows(v, t):
    return jnp.broadcast_to(v[t:t+1, :], (8, 128))

def factor128(a):
    lane = lax.broadcasted_iota(jnp.int32, (8, 128), 1)
    sub = lax.broadcasted_iota(jnp.int32, (8, 128), 0)
    a = list(a)
    w = [jnp.where(lane == sub + 8*i, 1.0, 0.0) for i in range(16)]
    fa, fw = [], []
    todo = []
    for b in range(16):
        x = [jnp.where(lane < 128 + k, lanes(a[b], 8*b+k), 1.0) for k in range(8)] + [a[b], w[b]]
        f = [None, None]
        share = -(-len(todo) // 4)
        for t in range(0, 8, 2):
            c0, c1 = x[t], x[t+1]
            p, q, s = rows(c0, t), rows(c0, t+1), rows(c1, t+1)
            det = p*s - q*q
            inv = 1.0 / det
            g0 = lax.rsqrt(p)
            g1 = p * lax.rsqrt(p * det)
            step = q * g0 * g0
            pi, qi, si = p*inv, q*inv, s*inv
            for k in range(t+2, 10):
                r0, r1 = rows(x[k], t), rows(x[k], t+1)
                if k >= 8:
                    y0, y1 = r0*g0, (r1 - step*r0)*g1
                    f[k-8] = jnp.where(sub == t, y0, y1) if t == 0 else jnp.where(sub < t, f[k-8], jnp.where(sub == t, y0, y1))
                u0, u1 = si*r0 - qi*r1, pi*r1 - qi*r0
                new = x[k] - (c0*u0 + c1*u1)
                x[k] = jnp.where(sub == t, u0, jnp.where(sub == t+1, u1, new))
            for work in todo[:share]: work()
            todo = todo[share:]
        for work in todo: work()
        fa.append(f[0]); fw.append(f[1])
        ga = [rows(x[8], k) for k in range(8)]
        gw = [rows(x[9], k) for k in range(8)]
        def update(i, b=b, ga=ga, gw=gw):
            c = [lanes(a[i], 8*b+k) for k in range(8)]
            a[i] = a[i] - tree([c[k]*ga[k] for k in range(8)])
            w[i] = w[i] - tree([c[k]*gw[k] for k in range(8)])
        if b < 15: update(b+1)
        todo = [functools.partial(update, i) for i in range(b+2, 16)]
    ro = [jnp.where(lane >= sub + 8*i, fa[i], 0.0) for i in range(16)]
    return ro, fw

def tree(v):
    while len(v) > 1: v = [v[n] + v[n+1] for n in range(0, len(v), 2)]
    return v[0]

def blocks(x): return [x[8*i:8*i+8, :] for i in range(x.shape[0]//8)]
def cat(bs): return jnp.concatenate(bs, axis=0)

def chol_kernel(scale, core_ref, own_ref, other_ref, c_ref, r_ref, p_ref):
    lane = lax.broadcasted_iota(jnp.int32, (128, 128), 1)
    sub = lax.broadcasted_iota(jnp.int32, (128, 128), 0)
    eye = lane == sub
    first = core_ref[0] == 0
    upper = sub[0:8] < 4
    tiles, tails = [], []
    for n in range(16):
        own, other = own_ref[n], other_ref[n]
        one, two = jnp.where(first, own, other), jnp.where(first, other, own)
        tiles += [one[0:8], two[0:8]]
        tails.append(jnp.where(upper, one[8:16], pltpu.roll(two[8:16], 4, 0)))
    a11, a21, a22 = cat(tiles[0:16]), cat(tiles[16:32]), cat(tails)
    def diag(x):
        e = jnp.where(eye, x, 0.0)
        return jnp.sum(e, axis=0, keepdims=True), jnp.sum(e, axis=1, keepdims=True)
    l1, s1 = diag(a11); l2, s2 = diag(a22)
    il1, is1, il2, is2 = map(lax.rsqrt, (l1, s1, l2, s2))
    c1, c2 = pltpu.roll(c_ref[...], 4, 0) * il1, pltpu.roll(c_ref[...], 2, 0) * il2
    a11 = a11 * is1 * il1
    a21 = a21 * is2 * il1
    a22 = a22 * is2 * il2
    r11, w1 = factor128(blocks(a11))
    r_ref[0:128, 0:128] = cat(r11) * (l1 * il1 * scale)
    w1 = cat(w1)
    low = nt(cat([a21, c1]), w1)
    l21, p1 = low[0:128], low[128:136]
    r_ref[0:128, 128:256] = nt(w1, a21) * (l2 * il2 * scale)
    upd = nt(low, l21)
    a22 = a22 - upd[0:128]
    c2 = c2 - upd[128:136]
    r22, w2 = factor128(blocks(a22))
    p2 = nt(c2, cat(w2))
    r_ref[128:256, 0:128] = jnp.zeros((128, 128), jnp.float32)
    r_ref[128:256, 128:256] = cat(r22) * (l2 * il2 * scale)
    p_ref[:, 0:128] = p1[0:2]
    p_ref[:, 128:256] = p2[0:2]

def chol(core, own, other, c, scale):
    vmem = pl.BlockSpec(memory_space=pltpu.VMEM)
    return pl.pallas_call(
        functools.partial(chol_kernel, scale),
        in_specs=[pl.BlockSpec(memory_space=pltpu.SMEM), vmem, vmem, vmem],
        out_shape=(jax.ShapeDtypeStruct((256, 256), jnp.float32), jax.ShapeDtypeStruct((2, 256), jnp.float32)),
        compiler_params=SMALL,
        name="factor",
    )(core, own, other, c)

GRAM_ROWS = 16
CROSS_ROWS = 64
PLANE = 16
RING = 16
ROWS = 2048
CHUNKS = 2
SMALL = pltpu.CompilerParams(vmem_limit_bytes=8 << 20)


def front_kernel(core_ref, deform_hbm, sketch_hbm, keep_ref, send_ref, deform, sketch, pair, lines, flat, sems):
    span = ROWS // CHUNKS
    load = pltpu.make_async_copy(sketch_hbm, sketch, sems.at[CHUNKS])
    load.start()
    loads = []
    for n in range(CHUNKS):
        part = pl.ds(n * span, span)
        loads.append(pltpu.make_async_copy(deform_hbm.at[part], deform.at[part], sems.at[n]))
        loads[-1].start()
    load.wait()
    flat[...] = sketch[...].T
    for n in range(CHUNKS):
        loads[n].wait()
        part = slice(n * span, (n + 1) * span)
        sketched = lax.dot_general(flat[...], deform[part], NT, preferred_element_type=jnp.float32)
        high = sketched.astype(jnp.bfloat16)
        pair[0:256, part] = high
        pair[256:512, part] = (sketched - high.astype(jnp.float32)).astype(jnp.bfloat16)
    gram = lax.dot_general(pair[...], pair[0:256, :], NT, preferred_element_type=jnp.float32)
    mixed = gram[256:512]
    whole = gram[0:256] + mixed + mixed.T
    packed = jnp.concatenate([whole[0:128, 0:128], whole[128:256, 0:128], whole[128:256, 128:256]], axis=0)
    core = core_ref[0]
    upper = lax.broadcasted_iota(jnp.int32, (8, 128), 0) < 4
    for peer in range(PLANE):
        one, two = packed[peer * 16 : peer * 16 + 8], packed[peer * 16 + 8 : peer * 16 + 16]
        tail = packed[256 + peer * 8 : 264 + peer * 8]
        turned = pltpu.roll(tail, 4, 0)
        keep_ref[peer, 0:8, :] = jnp.where(core == 0, one, two)
        send_ref[peer, 0:8, :] = jnp.where(core == 0, two, one)
        keep_ref[peer, 8:16, :] = jnp.where(upper, jnp.where(core == 0, tail, turned), 0.0)
        send_ref[peer, 8:16, :] = jnp.where(upper, jnp.where(core == 0, turned, tail), 0.0)
    for y in range(4):
        cols = slice(y * 256, y * 256 + 256)
        cross = jnp.dot(pair[...], deform[:, cols], preferred_element_type=jnp.float32)
        cross = cross[0:256] + cross[256:512]
        for half in range(2):
            for block in range(2):
                at = y * 256 + block * 128
                tile = cross[half * 128 : half * 128 + 128, block * 128 : block * 128 + 128]
                lines[half, at : at + 128, :] = tile.T
        for x in range(4):
            for half in range(2):
                for i in range(2):
                    at = GRAM_ROWS + (half * 2 + i) * RING
                    base = y * 256 + x * 4 + i
                    keep_ref[y * 4 + x, at : at + RING, :] = lines[half, pl.ds(base + core * 2, RING, stride=16), :]
                    send_ref[y * 4 + x, at : at + RING, :] = lines[half, pl.ds(base + 2 - core * 2, RING, stride=16), :]


def front(deform, sketch, core):
    shape = jax.ShapeDtypeStruct((PLANE, GRAM_ROWS + CROSS_ROWS, 128), jnp.float32)
    return pl.pallas_call(
        front_kernel,
        in_specs=[pl.BlockSpec(memory_space=pltpu.SMEM)] + [pl.BlockSpec(memory_space=pltpu.HBM)] * 2,
        out_specs=[pl.BlockSpec(memory_space=pltpu.VMEM)] * 2,
        scratch_shapes=[
            pltpu.VMEM((ROWS, 1024), jnp.bfloat16),
            pltpu.VMEM((1024, 256), jnp.bfloat16),
            pltpu.VMEM((512, ROWS), jnp.bfloat16),
            pltpu.VMEM((2, 1024, 128), jnp.float32),
            pltpu.VMEM((256, 1024), jnp.bfloat16),
            pltpu.SemaphoreType.DMA((CHUNKS + 1,)),
        ],
        out_shape=(shape, shape),
        compiler_params=pltpu.CompilerParams(vmem_limit_bytes=32 << 20),
        name="front",
    )(core, pltpu.with_memory_space_constraint(deform, pltpu.HBM), pltpu.with_memory_space_constraint(sketch, pltpu.HBM))


def plane_kernel(in_ref, out_ref):
    total = in_ref[0]
    for peer in range(1, PLANE):
        total = total + in_ref[peer]
    for z in range(RING):
        out_ref[z * 16 : z * 16 + 16, :] = total[0:GRAM_ROWS]
    for q in range(4):
        at = GRAM_ROWS + q * RING
        out_ref[pl.ds(12 + q, RING, stride=16), :] = total[at : at + RING]


def plane_sum(arrived):
    out = pl.pallas_call(
        plane_kernel,
        out_shape=jax.ShapeDtypeStruct((RING * 16, 128), jnp.float32),
        compiler_params=SMALL,
        name="plane_sum",
    )(arrived)
    return out.reshape(RING, 16, 128)


def ring_kernel(in_ref, chunk_ref, own_ref):
    total = in_ref[0]
    for z in range(1, RING):
        total = total + in_ref[z]
    for peer in range(PLANE):
        chunk_ref[peer] = total
    own_ref[...] = total[8:16]


def ring_sum(arrived):
    return pl.pallas_call(
        ring_kernel,
        out_shape=(
            jax.ShapeDtypeStruct((PLANE, GRAM_ROWS, 128), jnp.float32),
            jax.ShapeDtypeStruct((8, 128), jnp.float32),
        ),
        compiler_params=SMALL,
        name="ring_sum",
    )(arrived)


def swap(values, axis):
    return lax.all_to_all(values, axis, split_axis=0, concat_axis=0, tiled=True)


def body(deform, sketch):
    core = lax.axis_index("c").astype(jnp.int32).reshape(1)
    keep, send = front(deform, sketch, core)
    cores = [(0, 1), (1, 0)]
    chip = keep + lax.ppermute(send, "c", cores)
    own_plane = plane_sum(swap(chip, ("y", "x")))
    chunks, own = ring_sum(swap(own_plane, ("z",)))
    mine = swap(chunks, ("y", "x"))
    total_rows = deform.shape[0] * lax.axis_size(("y", "z", "x", "c"))
    return chol(core, mine, lax.ppermute(mine, "c", cores), own, 1.0 / float(np.sqrt(np.float32(total_rows))))


def solution(mesh):
    split = Mesh(mesh.devices.reshape(4, 16, 4, 2), ("y", "z", "x", "c"))
    axes = ("y", "z", "x", "c")
    in_specs = (P(axes, None), P())
    out_specs = (P(), P(axes, None))
    return jax.shard_map(body, mesh=split, in_specs=in_specs, out_specs=out_specs, check_vma=False)
```

```python
import functools

import jax
import jax.numpy as jnp
import numpy as np
from jax import lax
from jax.experimental import pallas as pl
from jax.experimental.pallas import tpu as pltpu
from jax.sharding import Mesh
from jax.sharding import PartitionSpec as P

NT = (((1,), (1,)), ((), ()))
def nt(a,b): return lax.dot_general(a,b,NT,precision=lax.Precision.HIGHEST,preferred_element_type=jnp.float32)

def lanes(v, k):
    return jnp.broadcast_to(v[:, k:k+1], (8, 128))
def rows(v, t):
    return jnp.broadcast_to(v[t:t+1, :], (8, 128))

def factor128(a):
    lane = lax.broadcasted_iota(jnp.int32, (8, 128), 1)
    sub = lax.broadcasted_iota(jnp.int32, (8, 128), 0)
    a = list(a)
    w = [jnp.where(lane == sub + 8*i, 1.0, 0.0) for i in range(16)]
    fa, fw = [], []
    todo = []
    for b in range(16):
        x = [jnp.where(lane < 128 + k, lanes(a[b], 8*b+k), 1.0) for k in range(8)] + [a[b], w[b]]
        f = [None, None]
        share = -(-len(todo) // 4)
        for t in range(0, 8, 2):
            c0, c1 = x[t], x[t+1]
            p, q, s = rows(c0, t), rows(c0, t+1), rows(c1, t+1)
            det = p*s - q*q
            inv = 1.0 / det
            g0 = lax.rsqrt(p)
            g1 = p * lax.rsqrt(p * det)
            step = q * g0 * g0
            pi, qi, si = p*inv, q*inv, s*inv
            for k in range(t+2, 10):
                r0, r1 = rows(x[k], t), rows(x[k], t+1)
                if k >= 8:
                    y0, y1 = r0*g0, (r1 - step*r0)*g1
                    f[k-8] = jnp.where(sub == t, y0, y1) if t == 0 else jnp.where(sub < t, f[k-8], jnp.where(sub == t, y0, y1))
                u0, u1 = si*r0 - qi*r1, pi*r1 - qi*r0
                new = x[k] - (c0*u0 + c1*u1)
                x[k] = jnp.where(sub == t, u0, jnp.where(sub == t+1, u1, new))
            for work in todo[:share]: work()
            todo = todo[share:]
        for work in todo: work()
        fa.append(f[0]); fw.append(f[1])
        ga = [rows(x[8], k) for k in range(8)]
        gw = [rows(x[9], k) for k in range(8)]
        def update(i, b=b, ga=ga, gw=gw):
            c = [lanes(a[i], 8*b+k) for k in range(8)]
            a[i] = a[i] - tree([c[k]*ga[k] for k in range(8)])
            w[i] = w[i] - tree([c[k]*gw[k] for k in range(8)])
        if b < 15: update(b+1)
        todo = [functools.partial(update, i) for i in range(b+2, 16)]
    ro = [jnp.where(lane >= sub + 8*i, fa[i], 0.0) for i in range(16)]
    return ro, fw

def tree(v):
    while len(v) > 1: v = [v[n] + v[n+1] for n in range(0, len(v), 2)]
    return v[0]

def blocks(x): return [x[8*i:8*i+8, :] for i in range(x.shape[0]//8)]
def cat(bs): return jnp.concatenate(bs, axis=0)

def chol_kernel(scale, g_ref, c_ref, r_ref, p_ref):
    lane = lax.broadcasted_iota(jnp.int32, (128, 128), 1)
    sub = lax.broadcasted_iota(jnp.int32, (128, 128), 0)
    eye = lane == sub
    upper = sub[0:8] < 4
    tiles = []
    for n in range(16):
        tiles += [g_ref[n, 0:8, :], g_ref[n, 8:16, :]]
    for n in range(8):
        tiles.append(jnp.where(upper, g_ref[2*n, 16:24, :], pltpu.roll(g_ref[2*n+1, 16:24, :], 4, 0)))
    corner = (sub < 64) & (lane >= 64)
    def mirrored(x):
        return jnp.where(corner, x.T, x)
    top = cat(tiles[0:8])
    a11 = mirrored(cat([top] + tiles[8:16]))
    a21 = cat(tiles[16:32])
    a22 = mirrored(cat([pltpu.roll(top, 64, 1)] + tiles[32:40]))
    def diag(x):
        e = jnp.where(eye, x, 0.0)
        return jnp.sum(e, axis=0, keepdims=True), jnp.sum(e, axis=1, keepdims=True)
    l1, s1 = diag(a11); l2, s2 = diag(a22)
    il1, is1, il2, is2 = map(lax.rsqrt, (l1, s1, l2, s2))
    c1, c2 = pltpu.roll(c_ref[...], 4, 0) * il1, pltpu.roll(c_ref[...], 2, 0) * il2
    a11 = a11 * is1 * il1
    a21 = a21 * is2 * il1
    a22 = a22 * is2 * il2
    r11, w1 = factor128(blocks(a11))
    r_ref[0:128, 0:128] = cat(r11) * (l1 * il1 * scale)
    w1 = cat(w1)
    low = nt(cat([a21, c1]), w1)
    l21, p1 = low[0:128], low[128:136]
    r_ref[0:128, 128:256] = nt(w1, a21) * (l2 * il2 * scale)
    upd = nt(low, l21)
    a22 = a22 - upd[0:128]
    c2 = c2 - upd[128:136]
    r22, w2 = factor128(blocks(a22))
    p2 = nt(c2, cat(w2))
    r_ref[128:256, 0:128] = jnp.zeros((128, 128), jnp.float32)
    r_ref[128:256, 128:256] = cat(r22) * (l2 * il2 * scale)
    p_ref[:, 0:128] = p1[0:2]
    p_ref[:, 128:256] = p2[0:2]

def chol(g, c, scale):
    return pl.pallas_call(
        functools.partial(chol_kernel, scale),
        out_shape=(jax.ShapeDtypeStruct((256, 256), jnp.float32), jax.ShapeDtypeStruct((2, 256), jnp.float32)),
        compiler_params=SMALL,
        name="factor",
    )(g, c)

GRAM_ROWS = 24
CROSS_ROWS = 64
PLANE = 16
RING = 16
ROWS = 2048
CHUNKS = 2
SMALL = pltpu.CompilerParams(vmem_limit_bytes=8 << 20)


def front_kernel(core_ref, deform_hbm, sketch_hbm, keep_ref, send_ref, deform, sketch, pair, lines, flat, sems):
    span = ROWS // CHUNKS
    load = pltpu.make_async_copy(sketch_hbm, sketch, sems.at[CHUNKS])
    load.start()
    loads = []
    for n in range(CHUNKS):
        part = pl.ds(n * span, span)
        loads.append(pltpu.make_async_copy(deform_hbm.at[part], deform.at[part], sems.at[n]))
        loads[-1].start()
    load.wait()
    flat[...] = sketch[...].T
    for n in range(CHUNKS):
        loads[n].wait()
        part = slice(n * span, (n + 1) * span)
        sketched = lax.dot_general(flat[...], deform[part], NT, preferred_element_type=jnp.float32)
        high = sketched.astype(jnp.bfloat16)
        pair[0:256, part] = high
        pair[256:512, part] = (sketched - high.astype(jnp.float32)).astype(jnp.bfloat16)
    gram = lax.dot_general(pair[...], pair[0:256, :], NT, preferred_element_type=jnp.float32)
    mixed = gram[256:512]
    whole = gram[0:256] + mixed + mixed.T
    core = core_ref[0]
    sub = lax.broadcasted_iota(jnp.int32, (8, 128), 0)
    low = lax.broadcasted_iota(jnp.int32, (64, 128), 1) < 64
    corners = jnp.where(low, whole[0:64, 0:128], pltpu.roll(whole[128:192, 128:256], 64, 1))
    packed = jnp.concatenate([corners, whole[64:128, 0:128], whole[128:256, 0:128], whole[192:256, 128:256]], axis=0)
    for peer in range(PLANE):
        tile = 256 + peer // 2 * 8
        tail = packed[tile : tile + 8]
        if peer % 2:
            tail = pltpu.roll(tail, 4, 0)
        for ref in (keep_ref, send_ref):
            ref[peer, 0:16, :] = packed[peer * 16 : peer * 16 + 16]
            ref[peer, 16:24, :] = jnp.where(sub < 4, tail, 0.0)
    for y in range(4):
        cols = slice(y * 256, y * 256 + 256)
        cross = jnp.dot(pair[...], deform[:, cols], preferred_element_type=jnp.float32)
        cross = cross[0:256] + cross[256:512]
        for half in range(2):
            for block in range(2):
                at = y * 256 + block * 128
                tile = cross[half * 128 : half * 128 + 128, block * 128 : block * 128 + 128]
                lines[half, at : at + 128, :] = tile.T
        for x in range(4):
            for half in range(2):
                for i in range(2):
                    at = GRAM_ROWS + (half * 2 + i) * RING
                    base = y * 256 + x * 4 + i
                    keep_ref[y * 4 + x, at : at + RING, :] = lines[half, pl.ds(base + core * 2, RING, stride=16), :]
                    send_ref[y * 4 + x, at : at + RING, :] = lines[half, pl.ds(base + 2 - core * 2, RING, stride=16), :]


def front(deform, sketch, core):
    shape = jax.ShapeDtypeStruct((PLANE, GRAM_ROWS + CROSS_ROWS, 128), jnp.float32)
    return pl.pallas_call(
        front_kernel,
        in_specs=[pl.BlockSpec(memory_space=pltpu.SMEM)] + [pl.BlockSpec(memory_space=pltpu.HBM)] * 2,
        out_specs=[pl.BlockSpec(memory_space=pltpu.VMEM)] * 2,
        scratch_shapes=[
            pltpu.VMEM((ROWS, 1024), jnp.bfloat16),
            pltpu.VMEM((1024, 256), jnp.bfloat16),
            pltpu.VMEM((512, ROWS), jnp.bfloat16),
            pltpu.VMEM((2, 1024, 128), jnp.float32),
            pltpu.VMEM((256, 1024), jnp.bfloat16),
            pltpu.SemaphoreType.DMA((CHUNKS + 1,)),
        ],
        out_shape=(shape, shape),
        compiler_params=pltpu.CompilerParams(vmem_limit_bytes=32 << 20),
        name="front",
    )(core, pltpu.with_memory_space_constraint(deform, pltpu.HBM), pltpu.with_memory_space_constraint(sketch, pltpu.HBM))


def plane_kernel(in_ref, out_ref):
    total = in_ref[0]
    for peer in range(1, PLANE):
        total = total + in_ref[peer]
    for z in range(RING):
        out_ref[z * 24 : z * 24 + 24, :] = total[0:GRAM_ROWS]
    for q in range(4):
        at = GRAM_ROWS + q * RING
        out_ref[pl.ds(20 + q, RING, stride=24), :] = total[at : at + RING]


def plane_sum(arrived):
    out = pl.pallas_call(
        plane_kernel,
        out_shape=jax.ShapeDtypeStruct((RING * 24, 128), jnp.float32),
        compiler_params=SMALL,
        name="plane_sum",
    )(arrived)
    return out.reshape(RING, 24, 128)


def ring_kernel(in_ref, chunk_ref, own_ref):
    total = in_ref[0]
    for z in range(1, RING):
        total = total + in_ref[z]
    for peer in range(PLANE):
        chunk_ref[peer] = total
    own_ref[...] = total[16:24]


def ring_sum(arrived):
    return pl.pallas_call(
        ring_kernel,
        out_shape=(
            jax.ShapeDtypeStruct((PLANE, GRAM_ROWS, 128), jnp.float32),
            jax.ShapeDtypeStruct((8, 128), jnp.float32),
        ),
        compiler_params=SMALL,
        name="ring_sum",
    )(arrived)


def swap(values, axis):
    return lax.all_to_all(values, axis, split_axis=0, concat_axis=0, tiled=True)


def body(deform, sketch):
    core = lax.axis_index("c").astype(jnp.int32).reshape(1)
    keep, send = front(deform, sketch, core)
    cores = [(0, 1), (1, 0)]
    chip = keep + lax.ppermute(send, "c", cores)
    own_plane = plane_sum(swap(chip, ("y", "x")))
    chunks, own = ring_sum(swap(own_plane, ("z",)))
    mine = swap(chunks, ("y", "x"))
    total_rows = deform.shape[0] * lax.axis_size(("y", "z", "x", "c"))
    return chol(mine, own, 1.0 / float(np.sqrt(np.float32(total_rows))))


def solution(mesh):
    split = Mesh(mesh.devices.reshape(4, 16, 4, 2), ("y", "z", "x", "c"))
    axes = ("y", "z", "x", "c")
    in_specs = (P(axes, None), P())
    out_specs = (P(), P(axes, None))
    return jax.shard_map(body, mesh=split, in_specs=in_specs, out_specs=out_specs, check_vma=False)
```

```python
import functools

import jax
import jax.numpy as jnp
import numpy as np
from jax import lax
from jax.experimental import pallas as pl
from jax.experimental.pallas import tpu as pltpu
from jax.sharding import Mesh
from jax.sharding import PartitionSpec as P

NT = (((1,), (1,)), ((), ()))
def nt(a,b): return lax.dot_general(a,b,NT,precision=lax.Precision.HIGHEST,preferred_element_type=jnp.float32)

def lanes(v, k):
    return jnp.broadcast_to(v[:, k:k+1], (8, 128))
def rows(v, t):
    return jnp.broadcast_to(v[t:t+1, :], (8, 128))

def factor128(a):
    lane = lax.broadcasted_iota(jnp.int32, (8, 128), 1)
    sub = lax.broadcasted_iota(jnp.int32, (8, 128), 0)
    a = list(a)
    w = [jnp.where(lane == sub + 8*i, 1.0, 0.0) for i in range(16)]
    fa, fw = [], []
    todo = []
    for b in range(16):
        x = [jnp.where(lane < 128 + k, lanes(a[b], 8*b+k), 1.0) for k in range(8)] + [a[b], w[b]]
        f = [None, None]
        share = -(-len(todo) // 4)
        for t in range(0, 8, 2):
            c0, c1 = x[t], x[t+1]
            p, q, s = rows(c0, t), rows(c0, t+1), rows(c1, t+1)
            det = p*s - q*q
            inv = 1.0 / det
            g0 = lax.rsqrt(p)
            g1 = p * lax.rsqrt(p * det)
            step = q * g0 * g0
            pi, qi, si = p*inv, q*inv, s*inv
            for k in range(t+2, 10):
                r0, r1 = rows(x[k], t), rows(x[k], t+1)
                if k >= 8:
                    y0, y1 = r0*g0, (r1 - step*r0)*g1
                    f[k-8] = jnp.where(sub == t, y0, y1) if t == 0 else jnp.where(sub < t, f[k-8], jnp.where(sub == t, y0, y1))
                u0, u1 = si*r0 - qi*r1, pi*r1 - qi*r0
                new = x[k] - (c0*u0 + c1*u1)
                x[k] = jnp.where(sub == t, u0, jnp.where(sub == t+1, u1, new))
            for work in todo[:share]: work()
            todo = todo[share:]
        for work in todo: work()
        fa.append(f[0]); fw.append(f[1])
        ga = [rows(x[8], k) for k in range(8)]
        gw = [rows(x[9], k) for k in range(8)]
        def update(i, b=b, ga=ga, gw=gw):
            c = [lanes(a[i], 8*b+k) for k in range(8)]
            a[i] = a[i] - tree([c[k]*ga[k] for k in range(8)])
            w[i] = w[i] - tree([c[k]*gw[k] for k in range(8)])
        if b < 15: update(b+1)
        todo = [functools.partial(update, i) for i in range(b+2, 16)]
    ro = [jnp.where(lane >= sub + 8*i, fa[i], 0.0) for i in range(16)]
    return ro, fw

def tree(v):
    while len(v) > 1: v = [v[n] + v[n+1] for n in range(0, len(v), 2)]
    return v[0]

def blocks(x): return [x[8*i:8*i+8, :] for i in range(x.shape[0]//8)]
def cat(bs): return jnp.concatenate(bs, axis=0)

def chol_kernel(scale, g_ref, c_ref, r_ref, p_ref):
    lane = lax.broadcasted_iota(jnp.int32, (128, 128), 1)
    sub = lax.broadcasted_iota(jnp.int32, (128, 128), 0)
    eye = lane == sub
    upper = sub[0:8] < 4
    tiles = []
    for n in range(16):
        tiles += [g_ref[n, 0:8, :], g_ref[n, 8:16, :]]
    for n in range(8):
        tiles.append(jnp.where(upper, g_ref[2*n, 16:24, :], pltpu.roll(g_ref[2*n+1, 16:24, :], 4, 0)))
    corner = (sub < 64) & (lane >= 64)
    def mirrored(x):
        return jnp.where(corner, x.T, x)
    top = cat(tiles[0:8])
    a11 = mirrored(cat([top] + tiles[8:16]))
    a21 = cat(tiles[16:32])
    a22 = mirrored(cat([pltpu.roll(top, 64, 1)] + tiles[32:40]))
    def diag(x):
        e = jnp.where(eye, x, 0.0)
        return jnp.sum(e, axis=0, keepdims=True), jnp.sum(e, axis=1, keepdims=True)
    l1, s1 = diag(a11); l2, s2 = diag(a22)
    il1, is1, il2, is2 = map(lax.rsqrt, (l1, s1, l2, s2))
    c1, c2 = pltpu.roll(c_ref[...], 4, 0) * il1, pltpu.roll(c_ref[...], 2, 0) * il2
    a11 = a11 * is1 * il1
    a21 = a21 * is2 * il1
    a22 = a22 * is2 * il2
    r11, w1 = factor128(blocks(a11))
    r_ref[0:128, 0:128] = cat(r11) * (l1 * il1 * scale)
    w1 = cat(w1)
    low = nt(cat([a21, c1]), w1)
    l21, p1 = low[0:128], low[128:136]
    r_ref[0:128, 128:256] = nt(w1, a21) * (l2 * il2 * scale)
    upd = nt(low, l21)
    a22 = a22 - upd[0:128]
    c2 = c2 - upd[128:136]
    r22, w2 = factor128(blocks(a22))
    p2 = nt(c2, cat(w2))
    r_ref[128:256, 0:128] = jnp.zeros((128, 128), jnp.float32)
    r_ref[128:256, 128:256] = cat(r22) * (l2 * il2 * scale)
    p_ref[:, 0:128] = p1[0:2]
    p_ref[:, 128:256] = p2[0:2]

def chol(g, c, scale):
    return pl.pallas_call(
        functools.partial(chol_kernel, scale),
        out_shape=(jax.ShapeDtypeStruct((256, 256), jnp.float32), jax.ShapeDtypeStruct((2, 256), jnp.float32)),
        compiler_params=SMALL,
        name="factor",
    )(g, c)

GRAM_ROWS = 24
CROSS_ROWS = 64
PLANE = 16
RING = 16
ROWS = 2048
CHUNKS = 2
SMALL = pltpu.CompilerParams(vmem_limit_bytes=8 << 20)


def front_kernel(core_ref, deform_hbm, sketch_hbm, keep_ref, send_ref, deform, sketch, pair, lines, flat, sems):
    span = ROWS // CHUNKS
    load = pltpu.make_async_copy(sketch_hbm, sketch, sems.at[CHUNKS])
    load.start()
    loads = []
    for n in range(CHUNKS):
        part = pl.ds(n * span, span)
        loads.append(pltpu.make_async_copy(deform_hbm.at[part], deform.at[part], sems.at[n]))
        loads[-1].start()
    load.wait()
    flat[...] = sketch[...].T
    for n in range(CHUNKS):
        loads[n].wait()
        part = slice(n * span, (n + 1) * span)
        sketched = lax.dot_general(flat[...], deform[part], NT, preferred_element_type=jnp.float32)
        high = sketched.astype(jnp.bfloat16)
        pair[0:256, part] = high
        pair[256:512, part] = (sketched - high.astype(jnp.float32)).astype(jnp.bfloat16)
    gram = lax.dot_general(pair[...], pair[0:256, :], NT, preferred_element_type=jnp.float32)
    mixed = gram[256:512]
    whole = gram[0:256] + mixed + mixed.T
    core = core_ref[0]
    sub = lax.broadcasted_iota(jnp.int32, (8, 128), 0)
    low = lax.broadcasted_iota(jnp.int32, (64, 128), 1) < 64
    corners = jnp.where(low, whole[0:64, 0:128], pltpu.roll(whole[128:192, 128:256], 64, 1))
    packed = jnp.concatenate([corners, whole[64:128, 0:128], whole[128:256, 0:128], whole[192:256, 128:256]], axis=0)
    for peer in range(PLANE):
        tile = 256 + peer // 2 * 8
        tail = packed[tile : tile + 8]
        if peer % 2:
            tail = pltpu.roll(tail, 4, 0)
        for ref in (keep_ref, send_ref):
            ref[peer, 0:16, :] = packed[peer * 16 : peer * 16 + 16]
            ref[peer, 16:24, :] = jnp.where(sub < 4, tail, 0.0)
    for y in range(4):
        cols = slice(y * 256, y * 256 + 256)
        cross = jnp.dot(pair[...], deform[:, cols], preferred_element_type=jnp.float32)
        cross = cross[0:256] + cross[256:512]
        for half in range(2):
            for block in range(2):
                at = y * 256 + block * 128
                tile = cross[half * 128 : half * 128 + 128, block * 128 : block * 128 + 128]
                lines[half, at : at + 128, :] = tile.T
        for x in range(4):
            for half in range(2):
                for i in range(2):
                    at = GRAM_ROWS + (half * 2 + i) * RING
                    base = y * 256 + x * 4 + i
                    keep_ref[x * 4 + y, at : at + RING, :] = lines[half, pl.ds(base + core * 2, RING, stride=16), :]
                    send_ref[x * 4 + y, at : at + RING, :] = lines[half, pl.ds(base + 2 - core * 2, RING, stride=16), :]


def front(deform, sketch, core):
    shape = jax.ShapeDtypeStruct((PLANE, GRAM_ROWS + CROSS_ROWS, 128), jnp.float32)
    return pl.pallas_call(
        front_kernel,
        in_specs=[pl.BlockSpec(memory_space=pltpu.SMEM)] + [pl.BlockSpec(memory_space=pltpu.HBM)] * 2,
        out_specs=[pl.BlockSpec(memory_space=pltpu.VMEM)] * 2,
        scratch_shapes=[
            pltpu.VMEM((ROWS, 1024), jnp.bfloat16),
            pltpu.VMEM((1024, 256), jnp.bfloat16),
            pltpu.VMEM((512, ROWS), jnp.bfloat16),
            pltpu.VMEM((2, 1024, 128), jnp.float32),
            pltpu.VMEM((256, 1024), jnp.bfloat16),
            pltpu.SemaphoreType.DMA((CHUNKS + 1,)),
        ],
        out_shape=(shape, shape),
        compiler_params=pltpu.CompilerParams(vmem_limit_bytes=32 << 20),
        name="front",
    )(core, pltpu.with_memory_space_constraint(deform, pltpu.HBM), pltpu.with_memory_space_constraint(sketch, pltpu.HBM))


def plane_kernel(in_ref, out_ref):
    total = in_ref[0]
    for peer in range(1, PLANE):
        total = total + in_ref[peer]
    for z in range(RING):
        out_ref[z * 24 : z * 24 + 24, :] = total[0:GRAM_ROWS]
    for q in range(4):
        at = GRAM_ROWS + q * RING
        out_ref[pl.ds(20 + q, RING, stride=24), :] = total[at : at + RING]


def plane_sum(arrived):
    out = pl.pallas_call(
        plane_kernel,
        out_shape=jax.ShapeDtypeStruct((RING * 24, 128), jnp.float32),
        compiler_params=SMALL,
        name="plane_sum",
    )(arrived)
    return out.reshape(RING, 24, 128)


def ring_kernel(in_ref, chunk_ref, own_ref):
    total = in_ref[0]
    for z in range(1, RING):
        total = total + in_ref[z]
    for peer in range(PLANE):
        chunk_ref[peer] = total
    own_ref[...] = total[16:24]


def ring_sum(arrived):
    return pl.pallas_call(
        ring_kernel,
        out_shape=(
            jax.ShapeDtypeStruct((PLANE, GRAM_ROWS, 128), jnp.float32),
            jax.ShapeDtypeStruct((8, 128), jnp.float32),
        ),
        compiler_params=SMALL,
        name="ring_sum",
    )(arrived)


def swap(values, axis):
    return lax.all_to_all(values, axis, split_axis=0, concat_axis=0, tiled=True)


def body(deform, sketch):
    core = lax.axis_index("c").astype(jnp.int32).reshape(1)
    keep, send = front(deform, sketch, core)
    cores = [(0, 1), (1, 0)]
    chip = keep + lax.ppermute(send, "c", cores)
    own_plane = plane_sum(swap(chip, ("x", "y")))
    chunks, own = ring_sum(swap(own_plane, ("z",)))
    mine = swap(chunks, ("x", "y"))
    total_rows = deform.shape[0] * lax.axis_size(("y", "z", "x", "c"))
    return chol(mine, own, 1.0 / float(np.sqrt(np.float32(total_rows))))


def solution(mesh):
    split = Mesh(mesh.devices.reshape(4, 16, 4, 2), ("y", "z", "x", "c"))
    axes = ("y", "z", "x", "c")
    in_specs = (P(axes, None), P())
    out_specs = (P(), P(axes, None))
    return jax.shard_map(body, mesh=split, in_specs=in_specs, out_specs=out_specs, check_vma=False)
```
